32 devices in a mesh: pipe: 2 (over x), dom: 8 (over z, y), rep: 2 (over core).
Axes of the slice: x: 2, y: 2, z: 4, core: 2. Of those that a mesh axis runs over, the one named last changes fastest.
Arguments:
- handoff: bfloat16 [2, 2, 4096, 512], P('pipe', 'rep', 'dom'), may hold values from -6 to 6
- initial: bfloat16 [2, 2, 4096, 512], P('pipe', 'rep', 'dom'), may hold values from -6 to 6
- cotangent: bfloat16 [2, 2, 4096, 512], P('pipe', 'rep', 'dom'), may hold values from -6 to 6
- slots: int32 [2, 2, 4096, 16], P('pipe', 'rep', 'dom'), may hold values from 0 to 639
- edge_weight: bfloat16 [2, 2, 4096, 16], P('pipe', 'rep', 'dom'), may hold values from 0.029907227 to 0.119628906
- boundary: int32 [2, 2, 8, 2, 64], P('pipe', 'rep', 'dom'), may hold values from 0 to 511
- weights: bfloat16 [4, 512, 512], P('pipe'), may hold values from -0.25 to 0.25
Outputs:
- section_out: bfloat16 [2, 2, 4096, 512], P('pipe', 'rep', 'dom')
- input_grad: bfloat16 [2, 2, 4096, 512], P('pipe', 'rep', 'dom')
- weight_grad: bfloat16 [4, 512, 512], P('pipe')
The draws below stay inside these ranges and needn't reach their ends.
All inputs are finite; a program needn't handle non-finite values.
Results may differ from the reference program's by a relative error of at most 0.013.
Values may be sent and summed in bfloat16 or wider, within the bound.
A program may use at most 64 MiB of HBM per device.

```python
import math
import jax
import jax.numpy as jnp

D = 512
K = 16
LAYERS = 2
ROWS = 512
BND = 64
NODES = 4096
N_PIPE = 2
N_DOM = 8
N_REP = 2


def touch_ends(values, rng, low, top_value):
    longest = values.shape.index(max(values.shape))
    spots = []
    for shift in (0, 1):
        where = [jax.random.randint(jax.random.fold_in(rng, axis), (), 0, length) for axis, length in enumerate(values.shape)]
        where[longest] = (where[longest] + shift) % values.shape[longest]
        spots.append(tuple(where))
    return values.at[spots[0]].set(low).at[spots[1]].set(top_value)


def shard_levels(own_key, shape, split, smallest, high):
    level, own = 1.0, jax.random.fold_in(own_key, 6)
    for axis_at, blocks in split:
        draws = jnp.exp(jax.random.uniform(jax.random.fold_in(own, axis_at), (blocks,), jnp.float32, smallest / len(split), high / len(split)))
        level = level * jnp.repeat(draws, shape[axis_at] // blocks).reshape([-1 if axis == axis_at else 1 for axis in range(len(shape))])
    return level


def bell_draw(own_key, dims, deviation, most, split=(), kind=jnp.bfloat16):
    drawn = jax.random.normal(own_key, dims, jnp.float32) * deviation
    if len(split) > 0:
        drawn = shard_levels(own_key, dims, split, -0.22, 0.18) * drawn
    return jnp.clip(drawn, min=-most, max=most).astype(kind)


def setup_inputs(seed: int = 0) -> dict:
    streams_of = jax.random.split(jax.random.key(seed), 8)
    handoff = bell_draw(streams_of[0], (N_PIPE, N_REP, NODES, D), 1.0, 6.0, ((0, 2), (1, 2), (2, 8)))
    initial = bell_draw(streams_of[1], (N_PIPE, N_REP, NODES, D), 1.0, 6.0, ((0, 2), (1, 2), (2, 8)))
    cotangent = bell_draw(streams_of[2], (N_PIPE, N_REP, NODES, D), 1.0, 6.0, ((0, 2), (1, 2), (2, 8)))
    slots = touch_ends(jax.random.randint(streams_of[3], (N_PIPE, N_REP, NODES, K), 0, ROWS + 2 * BND), jax.random.fold_in(streams_of[3], 1), 0, (ROWS + 2 * BND) - 1).astype(jnp.int32)
    edge_weight = jnp.clip(jnp.exp(math.log(0.119628906) - 1.3862944 * jax.random.uniform(streams_of[4], (N_PIPE, N_REP, NODES, K), jnp.float32) ** shard_levels(streams_of[4], (N_PIPE, N_REP, NODES, K), ((0, 2), (1, 2), (2, 8)), -0.2, 0.2)), 0.029907227, 0.119628906).astype(jnp.bfloat16)
    boundary = touch_ends(jax.random.randint(streams_of[5], (N_PIPE, N_REP, N_DOM, 2, BND), 0, ROWS), jax.random.fold_in(streams_of[5], 1), 0, ROWS - 1).astype(jnp.int32)
    weights = bell_draw(streams_of[6], (LAYERS * N_PIPE, D, D), D ** -0.5, 0.25, ((0, 2),))
    return {"handoff": handoff, "initial": initial, "cotangent": cotangent, "slots": slots, "edge_weight": edge_weight, "boundary": boundary, "weights": weights}


ALPHA = 0.1

def adjacency(slot_rows, weight_rows, width):
    columns = jnp.arange(width, dtype=jnp.int32)
    total = jnp.zeros((slot_rows.shape[0], width), jnp.float32)
    for k in range(slot_rows.shape[1]):
        total = total + jnp.where(slot_rows[:, k][:, None] == columns[None, :], weight_rows[:, k][:, None].astype(jnp.float32), jnp.float32(0.0))
    return total.astype(jnp.bfloat16)

def silu_slope(value):
    sig = jax.nn.sigmoid(value)
    return sig * (1.0 + value * (1.0 - sig))

def extend(rows, bound):
    to_prev = jax.vmap(lambda a, i: a[i])(rows, bound[:, 0])
    to_next = jax.vmap(lambda a, i: a[i])(rows, bound[:, 1])
    from_prev = jnp.roll(to_next, 1, axis=0)
    from_next = jnp.roll(to_prev, -1, axis=0)
    return jnp.concatenate([from_prev, rows, from_next], axis=1)

def retract(dext, bound):
    own = dext[:, BND:BND + ROWS]
    back_prev = dext[:, :BND]
    back_next = dext[:, BND + ROWS:]
    from_next = jnp.roll(back_prev, -1, axis=0)
    from_prev = jnp.roll(back_next, 1, axis=0)

    def place(base, index_prev, index_next, got_prev, got_next):
        return base.at[index_prev].add(got_prev).at[index_next].add(got_next)
    return jax.vmap(place)(own, bound[:, 0], bound[:, 1], from_prev, from_next)

def reference(handoff, initial, cotangent, slots, edge_weight, boundary, weights):
    npipe = N_PIPE
    ndom = N_DOM
    nrep = N_REP
    scale = 1.0 / math.sqrt(ROWS * ndom * nrep)
    f32 = jnp.float32
    outs_all = []
    grads_all = []
    wsums = [jnp.zeros((D, D), f32) for _ in range(LAYERS * npipe)]
    betas = [math.log(0.5 / (g + 1) + 1.0) for g in range(LAYERS * npipe)]
    for p in range(npipe):
        outs_row = []
        grads_row = []
        for r in range(nrep):
            state = handoff[(p - 1) % npipe, r].reshape(ndom, ROWS, D)
            start = initial[p, r].reshape(ndom, ROWS, D).astype(f32)
            adj = jax.vmap(lambda s, w: adjacency(s, w, ROWS + 2 * BND))(slots[p, r].reshape(ndom, ROWS, K), edge_weight[p, r].reshape(ndom, ROWS, K))
            bound = boundary[p, r]
            saved = []
            for layer in range(LAYERS):
                index = p * LAYERS + layer
                beta = betas[index]
                ext = extend(state, bound)
                agg = jnp.einsum('nrc,ncd->nrd', adj.astype(f32), ext.astype(f32))
                s_act = ((1.0 - ALPHA) * agg + ALPHA * start).astype(jnp.bfloat16)
                mixed = jnp.einsum('nrd,de->nre', s_act.astype(f32), weights[index].astype(f32))
                z_val = (1.0 - beta) * s_act.astype(f32) + beta * mixed
                state = jax.nn.silu(z_val).astype(jnp.bfloat16)
                saved.append((s_act, z_val))
            outs_row.append(state.reshape(ROWS * ndom, D))
            grad = cotangent[(p + 1) % npipe, r].reshape(ndom, ROWS, D)
            for layer in reversed(range(LAYERS)):
                index = p * LAYERS + layer
                beta = betas[index]
                s_act, z_val = saved[layer]
                dz_val = (grad.astype(f32) * silu_slope(z_val)).astype(jnp.bfloat16)
                wsums[index] = wsums[index] + jnp.einsum('nrd,nre->de', s_act.astype(f32), dz_val.astype(f32))
                back = jnp.einsum('nre,de->nrd', dz_val.astype(f32), weights[index].astype(f32))
                ds_val = (1.0 - beta) * dz_val.astype(f32) + beta * back
                dagg = ((1.0 - ALPHA) * ds_val).astype(jnp.bfloat16)
                dext = jnp.einsum('nrc,nrd->ncd', adj.astype(f32), dagg.astype(f32))
                grad = retract(dext, bound).astype(jnp.bfloat16)
            grads_row.append(grad.reshape(ROWS * ndom, D))
        outs_all.append(jnp.stack(outs_row))
        grads_all.append(jnp.stack(grads_row))
    weight_grad = jnp.stack([(betas[i] * scale * wsums[i]).astype(jnp.bfloat16) for i in range(LAYERS * npipe)])
    return (jnp.stack(outs_all), jnp.stack(grads_all), weight_grad)
```

```python
import functools
import math

import jax
import jax.numpy as jnp
from jax import lax
from jax.experimental import pallas as pl
from jax.experimental.pallas import tpu as pltpu
from jax.sharding import PartitionSpec as P

ALPHA = 0.1
BF = jnp.bfloat16
F32 = jnp.float32
PARTS = 2


def dot(a, b):
    return jnp.dot(a, b, preferred_element_type=F32)


def kernel(
    sizes,
    hand, init_h, cot, slots, ew, bnd, w_h,
    sec_out, in_grad, wg_out,
    x0, ct, init, w, wt, adj_o, adj_b, adjt_o, adjt_b, oh, oht,
    agg, s_act, s_t, slope, x1, x2, dz, dagg, own, gin,
    gsend, grecv, bsend, brecv,
    keep, asend, arecv, ysend, yrecv, tkeep, zsend, zrecv, wg,
    loc_sem, hs, hr, gs, gr, bs, br, a_s, a_r, y_s, y_r, z_s, z_r, q_s, q_r, f_s, f_r, e_s, e_r,
):
    npipe, ndom, nrep, rows, feat, width, layers = sizes
    nz = ndom // 2
    prow = feat // ndom
    half = feat // PARTS
    quart = half // nrep
    rb = 128
    blocks = rows // rb
    scale = 1.0 / math.sqrt(rows * ndom * nrep)

    pipe = lax.axis_index("pipe")
    dom = lax.axis_index("dom")
    rep = lax.axis_index("rep")
    z = dom // 2
    y = dom % 2

    def dev(p=pipe, d=dom, r=rep):
        return (p, d, r)

    pipe_next = dev(p=(pipe + 1) % npipe)
    pipe_prev = dev(p=(pipe + npipe - 1) % npipe)
    dom_next = dev(d=(dom + 1) % ndom)
    dom_prev = dev(d=(dom + ndom - 1) % ndom)
    twin = dev(d=z * 2 + (1 - y))
    mate = dev(r=1 - rep)
    z_peers = [dev(d=((z + k) % nz) * 2 + y) for k in range(1, nz)]

    def remote(src, dst, ss, rs, to):
        return pltpu.make_async_remote_copy(
            src_ref=src, dst_ref=dst, send_sem=ss, recv_sem=rs,
            device_id=to, device_id_type=pl.DeviceIdType.MESH,
        )

    barrier = pltpu.get_barrier_semaphore()
    greeted = [pipe_next, pipe_prev, dom_next, dom_prev, twin, mate] + z_peers
    for peer in greeted:
        pl.semaphore_signal(barrier, inc=1, device_id=peer, device_id_type=pl.DeviceIdType.MESH)
    load_w = pltpu.make_async_copy(w_h, w, loc_sem.at[0])
    load_i = pltpu.make_async_copy(init_h, init, loc_sem.at[1])
    load_w.start()
    load_i.start()
    pl.semaphore_wait(barrier, len(greeted))

    sends = []

    def go(copy):
        copy.start()
        sends.append(copy)
        return copy

    def cols(c):
        return pl.ds(c * half, half)

    hand_c = [
        go(remote(hand.at[:, cols(c)], x0.at[:, cols(c)], hs.at[0, c], hr.at[0, c], pipe_next))
        for c in range(PARTS)
    ]
    cot_c = [
        go(remote(cot.at[:, cols(c)], ct.at[:, cols(c)], hs.at[1, c], hr.at[1, c], pipe_prev))
        for c in range(PARTS)
    ]

    def loop(fn, n=blocks):
        def step(i, carry):
            fn(pl.ds(pl.multiple_of(i * rb, rb), rb))
            return carry
        lax.fori_loop(0, n, step, 0)

    betas = []
    for layer in range(layers):
        value = jnp.float32(0.0)
        for seg in range(npipe):
            value = jnp.where(
                pipe == seg, jnp.float32(math.log(0.5 / (seg * layers + layer + 1) + 1.0)), value
            )
        betas.append(value)

    def build(i, carry):
        rr = pl.ds(pl.multiple_of(i * 16, 16), 16)
        slot = slots[rr, :]
        wide = ew[rr, :].astype(F32)
        bslot = jnp.where(slot < width, slot, jnp.where(slot >= width + rows, slot - rows, -1))
        oslot = slot - width
        col_o = lax.broadcasted_iota(jnp.int32, (16, rows), 1)
        col_b = lax.broadcasted_iota(jnp.int32, (16, 2 * width), 1)
        tot_o = jnp.zeros((16, rows), F32)
        tot_b = jnp.zeros((16, 2 * width), F32)
        for k in range(slots.shape[1]):
            wk = wide[:, k : k + 1]
            tot_o = tot_o + jnp.where(oslot[:, k : k + 1] == col_o, wk, 0.0)
            tot_b = tot_b + jnp.where(bslot[:, k : k + 1] == col_b, wk, 0.0)
        adj_o[rr, :] = tot_o.astype(BF)
        adj_b[rr, :] = tot_b.astype(BF)
        return carry

    ids = jnp.concatenate([bnd[0:1, :], bnd[1:2, :]], axis=1)
    oht[...] = jnp.where(
        lax.broadcasted_iota(jnp.int32, (rows, 2 * width), 0) == ids, 1.0, 0.0
    ).astype(BF)
    oh[...] = oht[...].T
    lax.fori_loop(0, rows // 16, build, 0)
    adjt_o[...] = adj_o[...].T
    adjt_b[...] = adj_b[...].T
    load_w.wait()
    load_i.wait()
    for layer in range(layers):
        wt[layer] = w[layer].T

    lo, hi = pl.ds(0, width), pl.ds(width, width)

    def swap(send, recv, layer, cc, ss, rs, n):
        first = go(remote(send.at[layer, lo, cc], recv.at[layer, hi, cc], ss.at[n, 0], rs.at[n, 0], dom_prev))
        second = go(remote(send.at[layer, hi, cc], recv.at[layer, lo, cc], ss.at[n, 1], rs.at[n, 1], dom_next))
        return first, second

    def gather(x, layer, cc, n):
        gsend[layer, :, cc] = dot(oh[...], x[:, cc]).astype(BF)
        return swap(gsend, grecv, layer, cc, gs, gr, n)

    def agg_own(x, cc):
        def body(rr):
            agg[rr, cc] = dot(adj_o[rr, :], x[:, cc])
        loop(body)

    def agg_end(layer, cc):
        def body(rr):
            total = agg[rr, cc] + dot(adj_b[rr, :], grecv[layer, :, cc])
            s_act[layer, rr, cc] = (
                (1.0 - ALPHA) * total + ALPHA * init[rr, cc].astype(F32)
            ).astype(BF)
        loop(body)

    def mix(layer, out):
        beta = betas[layer]

        def body(rr):
            s = s_act[layer, rr, :]
            value = (1.0 - beta) * s.astype(F32) + beta * dot(s, w[layer])
            sig = jax.nn.sigmoid(value)
            out[rr, :] = (value * sig).astype(BF)
            slope[layer, rr, :] = sig * (1.0 + value * (1.0 - sig))
        loop(body)

    every = pl.ds(0, feat)
    for c in range(PARTS):
        hand_c[c].wait_recv()
        pair = gather(x0, 0, cols(c), c)
        agg_own(x0, cols(c))
        for copy in pair:
            copy.wait_recv()
        agg_end(0, cols(c))
    mix(0, x1)
    pair = gather(x1, 1, every, PARTS)
    agg_own(x1, every)
    s_t[0] = s_act[0].T
    for copy in pair:
        copy.wait_recv()
    agg_end(1, every)
    mix(1, x2)
    out_1 = pltpu.make_async_copy(x2, sec_out, loc_sem.at[2])
    out_1.start()
    s_t[1] = s_act[1].T

    def unit(layer, c):
        return (layers - 1 - layer) * PARTS + c

    def mine(c):
        return pl.ds(pl.multiple_of(c * half + rep * quart, quart), quart)

    def piece(zz, yy):
        return pl.ds(pl.multiple_of((zz * 2 + yy) * prow, prow), prow)

    live = {}

    def ar_a(layer, c):
        u = unit(layer, c)

        def body(rr):
            value = dot(s_t[layer, rr, :], dz[layer, :, cols(c)])
            left, right = value[:, :quart], value[:, quart:]
            keep[u, rr, :] = jnp.where(rep == 0, left, right)
            asend[u, rr, :] = jnp.where(rep == 0, right, left).astype(BF)
        loop(body, feat // rb)
        live["a", u] = go(remote(asend.at[u], arecv.at[u], a_s.at[u], a_r.at[u], mate))

    def ar_y(layer, c):
        u = unit(layer, c)
        live["a", u].wait_recv()
        for zz in range(nz):
            pp = piece(zz, 1 - y)
            ysend[u, zz] = (keep[u, pp, :] + arecv[u, pp, :].astype(F32)).astype(BF)
        live["y", u] = go(remote(ysend.at[u], yrecv.at[u], y_s.at[u], y_r.at[u], twin))
        for zz in range(nz):
            pp = piece(zz, y)
            tkeep[u, zz] = keep[u, pp, :] + arecv[u, pp, :].astype(F32)

    def ar_z(layer, c):
        u = unit(layer, c)
        live["y", u].wait_recv()
        live["z", u] = []
        for k in range(1, nz):
            zz = (z + k) % nz
            zsend[u, k - 1] = (tkeep[u, zz] + yrecv[u, zz].astype(F32)).astype(BF)
            live["z", u].append(
                go(remote(zsend.at[u, k - 1], zrecv.at[u, k - 1], z_s.at[u, k - 1], z_r.at[u, k - 1], z_peers[k - 1]))
            )

    def ar_g(layer, c):
        u = unit(layer, c)
        total = tkeep[u, z] + yrecv[u, z].astype(F32)
        for k in range(1, nz):
            live["z", u][k - 1].wait_recv()
            total = total + zrecv[u, k - 1].astype(F32)
        wg[layer, z, y, :, mine(c)] = (betas[layer] * scale * total).astype(BF)
        spot = wg.at[layer, z, y, :, mine(c)]
        live["q", u] = [
            go(remote(spot, spot, q_s.at[u, k], q_r.at[u, k], z_peers[k])) for k in range(nz - 1)
        ]

    def ar_f(layer, c):
        u = unit(layer, c)
        for copy in live["q", u]:
            copy.wait_recv()
        spot = wg.at[layer, :, y, :, mine(c)]
        live["f", u] = go(remote(spot, spot, f_s.at[u], f_r.at[u], twin))

    def ar_e(layer, c):
        u = unit(layer, c)
        live["f", u].wait_recv()
        spot = wg.at[layer, :, :, :, mine(c)]
        live["e", u] = go(remote(spot, spot, e_s.at[u], e_r.at[u], mate))

    def ar_end(layer, c):
        live["e", unit(layer, c)].wait_recv()

    def back(layer):
        beta = betas[layer]

        def body(rr):
            d = dz[layer, rr, :]
            ds_val = (1.0 - beta) * d.astype(F32) + beta * dot(d, wt[layer])
            dagg[layer, rr, :] = ((1.0 - ALPHA) * ds_val).astype(BF)
        loop(body)
        bsend[layer] = dot(adjt_b[...], dagg[layer]).astype(BF)
        return swap(bsend, brecv, layer, every, bs, br, layer)

    def dext_own(layer):
        def body(rr):
            own[rr, :] = dot(adjt_o[rr, :], dagg[layer])
        loop(body)

    last = layers - 1
    for c in range(PARTS):
        cot_c[c].wait_recv()

        def scaled(rr):
            dz[last, rr, cols(c)] = (ct[rr, cols(c)].astype(F32) * slope[last, rr, cols(c)]).astype(BF)
        loop(scaled)
        if c < PARTS - 1:
            ar_a(last, c)
            ar_y(last, c)
            ar_z(last, c)
    pair = back(1)
    ar_a(1, 1)
    dext_own(1)
    ar_y(1, 1)
    for copy in pair:
        copy.wait_recv()

    def inner(rr):
        grad = (own[rr, :] + dot(oht[rr, :], brecv[1])).astype(BF)
        dz[0, rr, :] = (grad.astype(F32) * slope[0, rr, :]).astype(BF)
    loop(inner)
    ar_a(0, 0)
    ar_a(0, 1)
    ar_g(1, 0)
    ar_y(0, 0)
    ar_y(0, 1)
    ar_z(1, 1)
    pair = back(0)
    ar_z(0, 0)
    ar_z(0, 1)
    ar_f(1, 0)
    dext_own(0)
    ar_g(1, 1)
    for copy in pair:
        copy.wait_recv()

    def final(rr):
        gin[rr, :] = (own[rr, :] + dot(oht[rr, :], brecv[0])).astype(BF)
    ar_g(0, 0)
    ar_g(0, 1)
    ar_f(1, 1)
    loop(final)
    out_2 = pltpu.make_async_copy(gin, in_grad, loc_sem.at[3])
    out_2.start()
    ar_e(1, 0)
    ar_f(0, 0)
    ar_f(0, 1)
    ar_e(1, 1)
    ar_e(0, 0)
    ar_e(0, 1)
    ar_end(1, 0)
    ar_end(1, 1)
    ar_end(0, 0)
    ar_end(0, 1)
    out_3 = pltpu.make_async_copy(wg, wg_out, loc_sem.at[4])
    out_3.start()
    for copy in sends:
        copy.wait_send()
    out_1.wait()
    out_2.wait()
    out_3.wait()


def local(sizes, handoff, initial, cotangent, slots, edge_weight, boundary, weights):
    npipe, ndom, nrep, rows, feat, width, layers = sizes
    nz = ndom // 2
    prow = feat // ndom
    quart = feat // PARTS // nrep
    units = layers * PARTS
    sem = pltpu.SemaphoreType.DMA
    vm = pltpu.VMEM
    square = (rows, feat)
    scratch = [
        vm(square, BF), vm(square, BF), vm(square, BF),
        vm((layers, feat, feat), BF), vm((layers, feat, feat), BF),
        vm((rows, rows), BF), vm((rows, 2 * width), BF),
        vm((rows, rows), BF), vm((2 * width, rows), BF),
        vm((2 * width, rows), BF), vm((rows, 2 * width), BF),
        vm(square, F32), vm((layers, rows, feat), BF), vm((layers, feat, rows), BF),
        vm((layers, rows, feat), F32), vm(square, BF), vm(square, BF),
        vm((layers, rows, feat), BF), vm((layers, rows, feat), BF), vm(square, F32), vm(square, BF),
        vm((layers, 2 * width, feat), BF), vm((layers, 2 * width, feat), BF),
        vm((layers, 2 * width, feat), BF), vm((layers, 2 * width, feat), BF),
        vm((units, feat, quart), F32), vm((units, feat, quart), BF), vm((units, feat, quart), BF),
        vm((units, nz, prow, quart), BF), vm((units, nz, prow, quart), BF),
        vm((units, nz, prow, quart), F32),
        vm((units, nz - 1, prow, quart), BF), vm((units, nz - 1, prow, quart), BF),
        vm((layers, nz, 2, prow, feat), BF),
        sem((5,)), sem((2, PARTS)), sem((2, PARTS)),
        sem((PARTS + 1, 2)), sem((PARTS + 1, 2)), sem((layers, 2)), sem((layers, 2)),
        sem((units,)), sem((units,)), sem((units,)), sem((units,)),
        sem((units, nz - 1)), sem((units, nz - 1)), sem((units, nz - 1)), sem((units, nz - 1)),
        sem((units,)), sem((units,)), sem((units,)), sem((units,)),
    ]
    anywhere = pl.BlockSpec(memory_space=pl.ANY)
    inside = pl.BlockSpec(memory_space=pltpu.VMEM)
    out, grad, wg = pl.pallas_call(
        functools.partial(kernel, sizes),
        out_shape=(
            jax.ShapeDtypeStruct(square, BF),
            jax.ShapeDtypeStruct(square, BF),
            jax.ShapeDtypeStruct((layers, nz, 2, prow, feat), BF),
        ),
        in_specs=[anywhere, anywhere, anywhere, inside, inside, inside, anywhere],
        out_specs=(anywhere, anywhere, anywhere),
        scratch_shapes=scratch,
        compiler_params=pltpu.CompilerParams(
            collective_id=0, has_side_effects=True, vmem_limit_bytes=48 * 1024 * 1024
        ),
        name="relay",
    )(
        handoff[0, 0], initial[0, 0], cotangent[0, 0], slots[0, 0], edge_weight[0, 0],
        boundary[0, 0, 0], weights,
    )
    return out[None, None], grad[None, None], wg.reshape(layers, feat, feat)


def solution(mesh):
    shape = dict(mesh.shape)
    specs = P("pipe", "rep", "dom", None)

    def whole(handoff, initial, cotangent, slots, edge_weight, boundary, weights):
        sizes = (
            shape["pipe"], shape["dom"], shape["rep"],
            handoff.shape[2] // shape["dom"], handoff.shape[3],
            boundary.shape[-1], weights.shape[0] // shape["pipe"],
        )
        return jax.shard_map(
            functools.partial(local, sizes),
            mesh=mesh,
            in_specs=(specs,) * 5 + (P("pipe", "rep", "dom", None, None), P("pipe", None, None)),
            out_specs=(specs, specs, P("pipe", None, None)),
            check_vma=False,
        )(handoff, initial, cotangent, slots, edge_weight, boundary, weights)

    return whole
```

```python
import contextlib
import functools
import math

import jax
import jax.numpy as jnp
from jax import lax
from jax.experimental import pallas as pl
from jax.experimental.pallas import tpu as pltpu
from jax.sharding import PartitionSpec as P

ALPHA = 0.1
BF = jnp.bfloat16
F32 = jnp.float32
PARTS = 2


def dot(a, b):
    return jnp.dot(a, b, preferred_element_type=F32)


def scope(name):
    return contextlib.nullcontext()


def kernel(
    sizes,
    hand, init_h, cot, slots_h, ew_h, bnd_h, w_h,
    sec_out, in_grad, wg_out,
    x2, gin, wg,
    slots, ew, bnd,
    x0, ct, init, w, wt, adj_o, adj_b, adjt_o, adjt_b, oh, oht,
    agg, s_act, s_t, slope, x1, dz, dagg, own,
    gsend, grecv, bsend, brecv,
    keep, asend, arecv, ysend, yrecv, tkeep, zsend, zrecv,
    loc_sem, hs, hr, gs, gr, bs, br, a_s, a_r, y_s, y_r, z_s, z_r, q_s, q_r, f_s, f_r, e_s, e_r,
):
    npipe, ndom, nrep, rows, feat, width, layers = sizes
    nz = ndom // 2
    prow = feat // ndom
    half = feat // PARTS
    quart = half // nrep
    rb = 128
    blocks = rows // rb
    scale = 1.0 / math.sqrt(rows * ndom * nrep)

    pipe = lax.axis_index("pipe")
    dom = lax.axis_index("dom")
    rep = lax.axis_index("rep")
    z = dom // 2
    y = dom % 2

    def dev(p=pipe, d=dom, r=rep):
        return (p, d, r)

    pipe_next = dev(p=(pipe + 1) % npipe)
    pipe_prev = dev(p=(pipe + npipe - 1) % npipe)
    dom_next = dev(d=(dom + 1) % ndom)
    dom_prev = dev(d=(dom + ndom - 1) % ndom)
    twin = dev(d=z * 2 + (1 - y))
    mate = dev(r=1 - rep)
    z_peers = [dev(d=((z + k) % nz) * 2 + y) for k in range(1, nz)]

    def remote(src, dst, ss, rs, to):
        return pltpu.make_async_remote_copy(
            src_ref=src, dst_ref=dst, send_sem=ss, recv_sem=rs,
            device_id=to, device_id_type=pl.DeviceIdType.MESH,
        )

    barrier = pltpu.get_barrier_semaphore()
    greeted = [pipe_next, pipe_prev, dom_next, dom_prev, twin, mate] + z_peers
    for peer in greeted:
        pl.semaphore_signal(barrier, inc=1, device_id=peer, device_id_type=pl.DeviceIdType.MESH)
    load_w = pltpu.make_async_copy(w_h, w, loc_sem.at[0])
    load_i = pltpu.make_async_copy(init_h, init, loc_sem.at[1])
    loads = [
        pltpu.make_async_copy(src, dst, loc_sem.at[2 + i])
        for i, (src, dst) in enumerate(((bnd_h, bnd), (slots_h, slots), (ew_h, ew)))
    ]
    for copy in loads:
        copy.start()
    load_w.start()
    load_i.start()
    pl.semaphore_wait(barrier, len(greeted))

    sends = []

    def go(copy):
        copy.start()
        sends.append(copy)
        return copy

    def cols(c):
        return pl.ds(c * half, half)

    hand_c = [
        go(remote(hand.at[:, cols(c)], x0.at[:, cols(c)], hs.at[0, c], hr.at[0, c], pipe_next))
        for c in range(PARTS)
    ]
    cot_c = [
        go(remote(cot.at[:, cols(c)], ct.at[:, cols(c)], hs.at[1, c], hr.at[1, c], pipe_prev))
        for c in range(PARTS)
    ]

    def loop(fn, n=blocks):
        def step(i, carry):
            fn(pl.ds(pl.multiple_of(i * rb, rb), rb))
            return carry
        lax.fori_loop(0, n, step, 0)

    betas = []
    for layer in range(layers):
        value = jnp.float32(0.0)
        for seg in range(npipe):
            value = jnp.where(
                pipe == seg, jnp.float32(math.log(0.5 / (seg * layers + layer + 1) + 1.0)), value
            )
        betas.append(value)

    def build(target, first):
        def body(i, carry):
            jj = pl.multiple_of(i * 16, 16)
            col = lax.broadcasted_iota(jnp.int32, (16, rows), 0) + first(jj)
            total = jnp.zeros((16, rows), F32)
            for k in range(slots.shape[0]):
                weight = ew[k : k + 1, :].astype(F32)
                total = total + jnp.where(slots[k : k + 1, :] == col, weight, 0.0)
            target[pl.ds(jj, 16), :] = total.astype(BF)
            return carry
        lax.fori_loop(0, target.shape[0] // 16, body, 0)

    for copy in loads:
        copy.wait()
    with scope("build"):
        ids = jnp.concatenate([bnd[0:1, :], bnd[1:2, :]], axis=1)
        oht[...] = jnp.where(
            lax.broadcasted_iota(jnp.int32, (rows, 2 * width), 0) == ids, 1.0, 0.0
        ).astype(BF)
        oh[...] = oht[...].T
        build(adjt_o, lambda jj: jj + width)
        build(adjt_b, lambda jj: jnp.where(jj < width, jj, jj + rows))
        adj_o[...] = adjt_o[...].T
        adj_b[...] = adjt_b[...].T
    load_w.wait()
    load_i.wait()
    for layer in range(layers):
        wt[layer] = w[layer].T

    lo, hi = pl.ds(0, width), pl.ds(width, width)

    def swap(send, recv, layer, cc, ss, rs, n):
        first = go(remote(send.at[layer, lo, cc], recv.at[layer, hi, cc], ss.at[n, 0], rs.at[n, 0], dom_prev))
        second = go(remote(send.at[layer, hi, cc], recv.at[layer, lo, cc], ss.at[n, 1], rs.at[n, 1], dom_next))
        return first, second

    def gather(x, layer, cc, n):
        gsend[layer, :, cc] = dot(oh[...], x[:, cc]).astype(BF)
        return swap(gsend, grecv, layer, cc, gs, gr, n)

    def agg_own(x, cc):
        def body(rr):
            agg[rr, cc] = dot(adj_o[rr, :], x[:, cc])
        loop(body)

    def agg_end(layer, cc):
        def body(rr):
            total = agg[rr, cc] + dot(adj_b[rr, :], grecv[layer, :, cc])
            s_act[layer, rr, cc] = (
                (1.0 - ALPHA) * total + ALPHA * init[rr, cc].astype(F32)
            ).astype(BF)
        loop(body)

    def mix(layer, out):
        beta = betas[layer]

        def body(rr):
            s = s_act[layer, rr, :]
            value = (1.0 - beta) * s.astype(F32) + beta * dot(s, w[layer])
            sig = jax.nn.sigmoid(value)
            out[rr, :] = (value * sig).astype(BF)
            slope[layer, rr, :] = sig * (1.0 + value * (1.0 - sig))
        loop(body)

    every = pl.ds(0, feat)
    for c in range(PARTS):
        hand_c[c].wait_recv()
        pair = gather(x0, 0, cols(c), c)
        agg_own(x0, cols(c))
        for copy in pair:
            copy.wait_recv()
        agg_end(0, cols(c))
    mix(0, x1)
    pair = gather(x1, 1, every, PARTS)
    agg_own(x1, every)
    s_t[0] = s_act[0].T
    for copy in pair:
        copy.wait_recv()
    agg_end(1, every)
    mix(1, x2)
    out_1 = pltpu.make_async_copy(x2, sec_out, loc_sem.at[5])
    out_1.start()
    s_t[1] = s_act[1].T

    def unit(layer, c):
        return (layers - 1 - layer) * PARTS + c

    def mine(c):
        return pl.ds(pl.multiple_of(c * half + rep * quart, quart), quart)

    def piece(zz, yy):
        return pl.ds(pl.multiple_of((zz * 2 + yy) * prow, prow), prow)

    live = {}

    def ar_a(layer, c):
        u = unit(layer, c)

        def body(rr):
            value = dot(s_t[layer, rr, :], dz[layer, :, cols(c)])
            left, right = value[:, :quart], value[:, quart:]
            keep[u, rr, :] = jnp.where(rep == 0, left, right)
            asend[u, rr, :] = jnp.where(rep == 0, right, left).astype(BF)
        loop(body, feat // rb)
        live["a", u] = go(remote(asend.at[u], arecv.at[u], a_s.at[u], a_r.at[u], mate))

    def ar_y(layer, c):
        u = unit(layer, c)
        live["a", u].wait_recv()
        for zz in range(nz):
            pp = piece(zz, 1 - y)
            ysend[u, zz] = (keep[u, pp, :] + arecv[u, pp, :].astype(F32)).astype(BF)
        live["y", u] = go(remote(ysend.at[u], yrecv.at[u], y_s.at[u], y_r.at[u], twin))
        for zz in range(nz):
            pp = piece(zz, y)
            tkeep[u, zz] = keep[u, pp, :] + arecv[u, pp, :].astype(F32)

    def ar_z(layer, c):
        u = unit(layer, c)
        live["y", u].wait_recv()
        live["z", u] = []
        for k in range(1, nz):
            zz = (z + k) % nz
            zsend[u, k - 1] = (tkeep[u, zz] + yrecv[u, zz].astype(F32)).astype(BF)
            live["z", u].append(
                go(remote(zsend.at[u, k - 1], zrecv.at[u, k - 1], z_s.at[u, k - 1], z_r.at[u, k - 1], z_peers[k - 1]))
            )

    def ar_g(layer, c):
        u = unit(layer, c)
        total = tkeep[u, z] + yrecv[u, z].astype(F32)
        for k in range(1, nz):
            live["z", u][k - 1].wait_recv()
            total = total + zrecv[u, k - 1].astype(F32)
        wg[layer, z, y, :, mine(c)] = (betas[layer] * scale * total).astype(BF)
        spot = wg.at[layer, z, y, :, mine(c)]
        live["q", u] = [
            go(remote(spot, spot, q_s.at[u, k], q_r.at[u, k], z_peers[k])) for k in range(nz - 1)
        ]

    def ar_f(layer, c):
        u = unit(layer, c)
        for copy in live["q", u]:
            copy.wait_recv()
        spot = wg.at[layer, :, y, :, mine(c)]
        live["f", u] = go(remote(spot, spot, f_s.at[u], f_r.at[u], twin))

    def ar_e(layer, c):
        u = unit(layer, c)
        live["f", u].wait_recv()
        spot = wg.at[layer, :, :, :, mine(c)]
        live["e", u] = go(remote(spot, spot, e_s.at[u], e_r.at[u], mate))

    def ar_end(layer, c):
        live["e", unit(layer, c)].wait_recv()

    def back(layer):
        beta = betas[layer]

        def body(rr):
            d = dz[layer, rr, :]
            ds_val = (1.0 - beta) * d.astype(F32) + beta * dot(d, wt[layer])
            dagg[layer, rr, :] = ((1.0 - ALPHA) * ds_val).astype(BF)
        loop(body)
        bsend[layer] = dot(adjt_b[...], dagg[layer]).astype(BF)
        return swap(bsend, brecv, layer, every, bs, br, layer)

    def dext_own(layer):
        def body(rr):
            own[rr, :] = dot(adjt_o[rr, :], dagg[layer])
        loop(body)

    last = layers - 1
    for c in range(PARTS):
        cot_c[c].wait_recv()

        def scaled(rr):
            dz[last, rr, cols(c)] = (ct[rr, cols(c)].astype(F32) * slope[last, rr, cols(c)]).astype(BF)
        loop(scaled)
        if c < PARTS - 1:
            ar_a(last, c)
    pair = back(1)
    ar_a(1, 1)
    ar_y(1, 0)
    dext_own(1)
    ar_y(1, 1)
    for copy in pair:
        copy.wait_recv()

    def inner(rr):
        grad = (own[rr, :] + dot(oht[rr, :], brecv[1])).astype(BF)
        dz[0, rr, :] = (grad.astype(F32) * slope[0, rr, :]).astype(BF)
    loop(inner)
    ar_a(0, 0)
    ar_a(0, 1)
    ar_z(1, 0)
    ar_y(0, 0)
    ar_z(1, 1)
    ar_y(0, 1)
    pair = back(0)
    ar_g(1, 0)
    ar_g(1, 1)
    ar_z(0, 0)
    dext_own(0)
    ar_z(0, 1)
    ar_f(1, 0)
    ar_f(1, 1)
    for copy in pair:
        copy.wait_recv()

    def final(rr):
        gin[rr, :] = (own[rr, :] + dot(oht[rr, :], brecv[0])).astype(BF)
    ar_g(0, 0)
    ar_g(0, 1)
    loop(final)
    out_2 = pltpu.make_async_copy(gin, in_grad, loc_sem.at[6])
    out_2.start()
    ar_e(1, 0)
    ar_e(1, 1)
    ar_f(0, 0)
    ar_f(0, 1)
    ar_end(1, 0)
    ar_end(1, 1)
    out_3 = pltpu.make_async_copy(wg.at[1], wg_out.at[1], loc_sem.at[7])
    out_3.start()
    ar_e(0, 0)
    ar_e(0, 1)
    ar_end(0, 0)
    ar_end(0, 1)
    out_4 = pltpu.make_async_copy(wg.at[0], wg_out.at[0], loc_sem.at[8])
    out_4.start()
    for copy in (out_1, out_2, out_3, out_4):
        copy.wait()
    for copy in sends:
        copy.wait_send()


def put_out(a, b, c, a_out, b_out, c_out, a_mid, b_mid, c_mid, sems):
    loads, stores = [], []
    for i, (src, mid, dst) in enumerate(((a, a_mid, a_out), (b, b_mid, b_out), (c, c_mid, c_out))):
        loads.append(pltpu.make_async_copy(src, mid, sems.at[0, i]))
        stores.append(pltpu.make_async_copy(mid, dst, sems.at[1, i]))
    for load in loads:
        load.start()
    for load, store in zip(loads, stores):
        load.wait()
        store.start()
    for store in stores:
        store.wait()


def local(sizes, handoff, initial, cotangent, slots, edge_weight, boundary, weights):
    npipe, ndom, nrep, rows, feat, width, layers = sizes
    nz = ndom // 2
    prow = feat // ndom
    quart = feat // PARTS // nrep
    units = layers * PARTS
    sem = pltpu.SemaphoreType.DMA
    vm = pltpu.VMEM
    square = (rows, feat)
    taps = slots.shape[-1]
    scratch = [
        vm(square, BF), vm(square, BF), vm((layers, nz, 2, prow, feat), BF),
        vm((taps, rows), jnp.int32), vm((taps, rows), BF), vm((2, width), jnp.int32),
        vm(square, BF), vm(square, BF), vm(square, BF),
        vm((layers, feat, feat), BF), vm((layers, feat, feat), BF),
        vm((rows, rows), BF), vm((rows, 2 * width), BF),
        vm((rows, rows), BF), vm((2 * width, rows), BF),
        vm((2 * width, rows), BF), vm((rows, 2 * width), BF),
        vm(square, F32), vm((layers, rows, feat), BF), vm((layers, feat, rows), BF),
        vm((layers, rows, feat), F32), vm(square, BF),
        vm((layers, rows, feat), BF), vm((layers, rows, feat), BF), vm(square, F32),
        vm((layers, 2 * width, feat), BF), vm((layers, 2 * width, feat), BF),
        vm((layers, 2 * width, feat), BF), vm((layers, 2 * width, feat), BF),
        vm((units, feat, quart), F32), vm((units, feat, quart), BF), vm((units, feat, quart), BF),
        vm((units, nz, prow, quart), BF), vm((units, nz, prow, quart), BF),
        vm((units, nz, prow, quart), F32),
        vm((units, nz - 1, prow, quart), BF), vm((units, nz - 1, prow, quart), BF),
        sem((9,)), sem((2, PARTS)), sem((2, PARTS)),
        sem((PARTS + 1, 2)), sem((PARTS + 1, 2)), sem((layers, 2)), sem((layers, 2)),
        sem((units,)), sem((units,)), sem((units,)), sem((units,)),
        sem((units, nz - 1)), sem((units, nz - 1)), sem((units, nz - 1)), sem((units, nz - 1)),
        sem((units,)), sem((units,)), sem((units,)), sem((units,)),
    ]
    far = pl.BlockSpec(memory_space=pltpu.HBM)
    shapes = (
        jax.ShapeDtypeStruct(square, BF),
        jax.ShapeDtypeStruct(square, BF),
        jax.ShapeDtypeStruct((layers, nz, 2, prow, feat), BF),
    )
    made = pl.pallas_call(
        functools.partial(kernel, sizes),
        out_shape=shapes,
        in_specs=[far] * 7,
        out_specs=(far,) * 3,
        scratch_shapes=scratch,
        compiler_params=pltpu.CompilerParams(
            collective_id=0, has_side_effects=True, vmem_limit_bytes=60 * 1024 * 1024
        ),
        name="relay",
    )(
        handoff[0, 0], initial[0, 0], cotangent[0, 0], slots[0, 0].T, edge_weight[0, 0].T,
        boundary[0, 0, 0], weights,
    )
    out, grad, wg = pl.pallas_call(
        put_out,
        out_shape=shapes,
        in_specs=[far] * 3,
        out_specs=(far,) * 3,
        scratch_shapes=[vm(one.shape, BF) for one in shapes] + [sem((2, 3))],
        compiler_params=pltpu.CompilerParams(vmem_limit_bytes=60 * 1024 * 1024),
        name="put_out",
    )(*made)
    return out[None, None], grad[None, None], wg.reshape(layers, feat, feat)


def solution(mesh):
    shape = dict(mesh.shape)
    specs = P("pipe", "rep", "dom", None)

    def whole(handoff, initial, cotangent, slots, edge_weight, boundary, weights):
        sizes = (
            shape["pipe"], shape["dom"], shape["rep"],
            handoff.shape[2] // shape["dom"], handoff.shape[3],
            boundary.shape[-1], weights.shape[0] // shape["pipe"],
        )
        return jax.shard_map(
            functools.partial(local, sizes),
            mesh=mesh,
            in_specs=(specs,) * 5 + (P("pipe", "rep", "dom", None, None), P("pipe", None, None)),
            out_specs=(specs, specs, P("pipe", None, None)),
            check_vma=False,
        )(handoff, initial, cotangent, slots, edge_weight, boundary, weights)

    return whole
```
